512 devices in a mesh: section: 2 (over y_lo), hid: 16 (over z), wid: 16 (over x, y_hi, core).
Axes of the slice: x: 4, y: 4 (y_hi: 2, y_lo: 2; y = y_hi * 2 + y_lo), z: 16, core: 2. Of those that a mesh axis runs over, the one named last changes fastest.
Arguments:
- weights: bfloat16 [2, 6144, 24576], P('section', 'hid', 'wid'), may hold values from -0.078125 to 0.078125
- preact: bfloat16 [1024, 24576], P(('section', 'hid'), 'wid'), may hold values from -6 to 6
- inputs: bfloat16 [1024, 6144], P(('section', 'wid'), 'hid'), may hold values from -6 to 6
- grad_out: bfloat16 [1024, 6144], P(('section', 'wid'), 'hid'), may hold values from -6 to 6
- row_state: float32 [2, 6144], P('section', 'hid'), may hold values from 32 to 256
- col_state: float32 [2, 24576], P('section', 'wid'), may hold values from 32 to 256
Outputs:
- input_grad: float32 [1024, 6144], P(('section', 'wid'), 'hid')
- update: float32 [2, 6144, 24576], P('section', 'hid', 'wid')
The draws below stay inside these ranges and needn't reach their ends.
All inputs are finite; a program needn't handle non-finite values.
Results may differ from the reference program's by a relative error of at most 0.0029.
Values may be sent and summed in bfloat16 or wider, within the bound.
No kernel may reach another device: no remote copies, remote signals or barrier semaphores. Data moves between devices by JAX's collectives and lax.ppermute only.
A program may use at most 64 MiB of HBM per device.

```python
import math
import jax
import jax.numpy as jnp
from jax import lax

D = 6144
FF = 24576
TOKENS = 1024


def block_scale(rng, shape, cuts, low, top_value):
    factor_of, own = 1.0, jax.random.fold_in(rng, 6)
    for dim, parts in cuts:
        draws = jnp.exp(jax.random.uniform(jax.random.fold_in(own, dim), (parts,), jnp.float32, low / len(cuts), top_value / len(cuts)))
        factor_of = factor_of * jnp.repeat(draws, shape[dim] // parts).reshape([-1 if axis == dim else 1 for axis in range(len(shape))])
    return factor_of


def normal_values(key, extent, scale, bound, split=(), kind=jnp.bfloat16):
    drawn = jax.random.normal(key, extent, jnp.float32) * scale
    if len(split) > 0:
        drawn = block_scale(key, extent, split, -0.22, 0.18) * drawn
    return jnp.clip(drawn, min=-bound, max=bound).astype(kind)


def setup_inputs(seed: int = 0) -> dict:
    keys = jax.random.split(jax.random.key(seed), 7)
    return {
        "weights": normal_values(keys[0], (2, D, FF), D ** -0.5, 0.078125, ((0, 2), (1, 16), (2, 16))),
        "preact": normal_values(keys[1], (TOKENS, FF), 1.0, 6.0, ((0, 32), (1, 16))),
        "inputs": normal_values(keys[2], (TOKENS, D), 1.0, 6.0, ((0, 32), (1, 16))),
        "grad_out": normal_values(keys[3], (TOKENS, D), 1.0, 6.0, ((0, 32), (1, 16))),
        "row_state": jnp.clip(jnp.exp(math.log(256.0) - 2.0794415 * jax.random.uniform(keys[4], (2, D), jnp.float32) ** block_scale(keys[4], (2, D), ((0, 2), (1, 16)), -0.2, 0.2)), 32.0, 256.0),
        "col_state": jnp.clip(jnp.exp(math.log(256.0) - 2.0794415 * jax.random.uniform(keys[5], (2, FF), jnp.float32) ** block_scale(keys[5], (2, FF), ((0, 2), (1, 16)), -0.2, 0.2)), 32.0, 256.0),
    }


decay_rate = 0.9
root_half = 0.7071067811865476
inv_root_tau = 0.3989422804014327

def normal_cdf(pre):
    return 0.5 * (1.0 + lax.erf(pre * root_half))

def gelu_value(pre):
    return pre * normal_cdf(pre)

def gelu_slope(pre):
    return normal_cdf(pre) + pre * jnp.exp(-0.5 * pre * pre) * inv_root_tau

def factored_step(gradient, row_prev, col_prev):
    squares = gradient * gradient
    row_moment = decay_rate * row_prev + (1.0 - decay_rate) * lax.optimization_barrier(jnp.mean(squares, axis=1))
    col_moment = decay_rate * col_prev + (1.0 - decay_rate) * lax.optimization_barrier(jnp.mean(squares, axis=0))
    second = row_moment[:, None] * col_moment[None, :] / jnp.mean(row_moment)
    return gradient * lax.rsqrt(second)

def reference(weights, preact, inputs, grad_out, row_state, col_state):
    pre_float = preact.astype(jnp.float32)
    activation = gelu_value(pre_float).astype(jnp.bfloat16)
    down_grad = lax.dot_general(grad_out, activation, (((0,), (0,)), ((), ())), preferred_element_type=jnp.float32)
    hidden_grad = jnp.dot(grad_out, weights[1], preferred_element_type=jnp.float32)
    pre_grad = (hidden_grad * gelu_slope(pre_float)).astype(jnp.bfloat16)
    up_grad = lax.dot_general(inputs, pre_grad, (((0,), (0,)), ((), ())), preferred_element_type=jnp.float32)
    input_grad = lax.dot_general(pre_grad, weights[0], (((1,), (1,)), ((), ())), preferred_element_type=jnp.float32)
    input_grad = input_grad + grad_out.astype(jnp.float32)
    first_step = factored_step(up_grad, row_state[0], col_state[0])
    second_step = factored_step(down_grad, row_state[1], col_state[1])
    return (input_grad, jnp.stack([first_step, second_step]))
```

```python
import jax
import jax.numpy as jnp
from jax import lax
from jax.sharding import PartitionSpec as P

D = 6144
FF = 24576


decay_rate = 0.9
root_half = 0.7071067811865476
inv_root_tau = 0.3989422804014327
LANES = 128


def normal_cdf(pre):
    return 0.5 * (1.0 + lax.erf(pre * root_half))


def gelu_value(pre):
    return pre * normal_cdf(pre)


def gelu_slope(pre):
    return normal_cdf(pre) + pre * jnp.exp(-0.5 * pre * pre) * inv_root_tau


def contract(left, right):
    return lax.dot_general(
        left, right, (((0,), (0,)), ((), ())), preferred_element_type=jnp.float32
    )


def exchange(blocks, axis):
    return lax.all_to_all(blocks, axis, split_axis=0, concat_axis=0, tiled=True)


def spread(block, axis):
    n = lax.axis_size(axis)
    copies = jnp.broadcast_to(block[None], (n,) + block.shape)
    return exchange(copies.reshape((n * block.shape[0],) + block.shape[1:]), axis)


def shards(weights, preact, inputs, grad_out, row_state, col_state):
    hid = lax.axis_size("hid")
    wid = lax.axis_size("wid")
    own_tile = weights[0]
    features, hidden = own_tile.shape
    rows = grad_out.shape[0]
    first = lax.axis_index("section") == 0

    kept = jnp.where(first, inputs, grad_out)
    given = jnp.where(first, grad_out, inputs)
    taken = lax.ppermute(given, "section", [(0, 1), (1, 0)])
    pre_taken = lax.ppermute(preact, "section", [(0, 1), (1, 0)])
    left_own = jnp.concatenate([jnp.where(first, kept, taken), jnp.where(first, taken, kept)])
    left = spread(left_own, "wid")

    hidden_share = lax.psum_scatter(
        jnp.dot(left, own_tile, preferred_element_type=jnp.float32),
        "hid",
        scatter_dimension=0,
        tiled=True,
    )
    pre_pair = jnp.concatenate(
        [jnp.where(first, preact, pre_taken), jnp.where(first, pre_taken, preact)]
    ).astype(jnp.float32)
    pre_share = (hidden_share * gelu_slope(pre_pair)).astype(jnp.bfloat16)
    pre_share = lax.ppermute(pre_share, "section", [(1, 0)])
    act_share = gelu_value(pre_pair).astype(jnp.bfloat16)
    right = lax.all_gather(jnp.where(first, pre_share, act_share), "hid", axis=0, tiled=True)

    gradient = contract(left, right)
    squares = gradient * gradient
    row_local = jnp.sum(squares, axis=1)
    col_local = jnp.sum(squares, axis=0)
    row_prev = row_state[0]
    col_prev = col_state[0]
    scalars = jnp.stack([jnp.sum(row_local), jnp.sum(row_prev)])
    tail = jnp.concatenate([scalars, jnp.zeros((4 * LANES - 2,), jnp.float32)])
    packed = jnp.concatenate([col_local, tail]).reshape(-1, LANES)
    over_hid = jnp.sum(
        spread(packed, "hid").reshape((hid,) + packed.shape), axis=0
    ).reshape(-1)
    col_total = over_hid[:hidden]
    square_sum, prev_sum = over_hid[hidden], over_hid[hidden + 1]

    partial = lax.dot_general(
        right, own_tile, (((1,), (1,)), ((), ())), preferred_element_type=jnp.float32
    )
    extra = jnp.concatenate(
        [row_local[None], jnp.broadcast_to(square_sum, (1, features)), jnp.zeros((6, features), jnp.float32)]
    )
    blocks = jnp.concatenate(
        [partial.reshape(wid, 2 * rows, features), jnp.broadcast_to(extra[None], (wid,) + extra.shape)],
        axis=1,
    )
    over_wid = jnp.sum(
        exchange(blocks.reshape(-1, features), "wid").reshape(blocks.shape), axis=0
    )
    input_sum = jnp.where(
        first, over_wid[:rows], lax.ppermute(over_wid[rows : 2 * rows], "section", [(0, 1)])
    )
    input_grad = input_sum + grad_out.astype(jnp.float32)

    row_total = over_wid[2 * rows]
    square_total = over_wid[2 * rows + 1, 0]
    row_moment = decay_rate * row_prev + (1.0 - decay_rate) / FF * row_total
    col_moment = decay_rate * col_prev + (1.0 - decay_rate) / D * col_total
    row_mean = decay_rate / D * prev_sum + (1.0 - decay_rate) / FF / D * square_total
    update = gradient * lax.rsqrt(row_moment[:, None] * col_moment[None, :] / row_mean)
    return (input_grad, update[None])


def solution(mesh):
    placed = (
        P("section", "hid", "wid"),
        P(("section", "hid"), "wid"),
        P(("section", "wid"), "hid"),
        P(("section", "wid"), "hid"),
        P("section", "hid"),
        P("section", "wid"),
    )
    return jax.shard_map(
        shards,
        mesh=mesh,
        in_specs=placed,
        out_specs=(P(("section", "wid"), "hid"), P("section", "hid", "wid")),
        check_vma=False,
    )
```

```python
import jax
import jax.numpy as jnp
from jax import lax
from jax.sharding import PartitionSpec as P

D = 6144
FF = 24576


decay_rate = 0.9
root_half = 0.7071067811865476
inv_root_tau = 0.3989422804014327
LANES = 128


def normal_cdf(pre):
    return 0.5 * (1.0 + lax.erf(pre * root_half))


def gelu_value(pre):
    return pre * normal_cdf(pre)


def gelu_slope(pre):
    return normal_cdf(pre) + pre * jnp.exp(-0.5 * pre * pre) * inv_root_tau


def contract(left, right):
    return lax.dot_general(
        left, right, (((0,), (0,)), ((), ())), preferred_element_type=jnp.float32
    )


def exchange(blocks, axis):
    return lax.all_to_all(blocks, axis, split_axis=0, concat_axis=0, tiled=True)


def spread(block, axis):
    n = lax.axis_size(axis)
    copies = jnp.broadcast_to(block[None], (n,) + block.shape)
    return exchange(copies.reshape((n * block.shape[0],) + block.shape[1:]), axis)


def thirds(values, scalar):
    shape = (16, values.shape[0])
    row = lax.broadcasted_iota(jnp.int32, shape, 0)
    rest = jnp.where(row < 8, jnp.broadcast_to(values[None], shape), scalar)
    out = jnp.zeros(shape, jnp.float32)
    for k in range(3):
        term = lax.reduce_precision(rest, exponent_bits=8, mantissa_bits=7)
        out = jnp.where(row % 8 == k, term, out)
        rest = rest - term
    return out.astype(jnp.bfloat16)


def shards(weights, preact, inputs, grad_out, row_state, col_state):
    hid = lax.axis_size("hid")
    wid = lax.axis_size("wid")
    own_tile = weights[0]
    features, hidden = own_tile.shape
    rows = grad_out.shape[0]
    first = lax.axis_index("section") == 0
    even = lax.axis_index("hid") % 2 == 0
    pair = ("section", "hid")
    evens = range(0, hid, 2)
    down = [(h, hid + h) for h in evens]
    across = [(h + 1, hid + h) for h in evens] + [(hid + h, hid + h + 1) for h in evens]
    swap = [(hid + h, hid + (h ^ 1)) for h in range(hid)]
    rings = [list(range(p, hid, 2)) for p in range(2)]

    grad_down = lax.ppermute(grad_out, pair, down)
    grad_across = lax.ppermute(grad_out, pair, across)
    next_tile = lax.ppermute(own_tile, pair, swap)
    grad_pair = jnp.concatenate([jnp.where(even, grad_down, grad_out), grad_across], axis=1)
    grad_half = spread(grad_pair, "wid")
    hidden_part = jnp.dot(
        grad_half[:, :features], own_tile, preferred_element_type=jnp.float32
    ) + jnp.dot(grad_half[:, features:], next_tile, preferred_element_type=jnp.float32)
    hidden_share = lax.psum_scatter(
        hidden_part, "hid", scatter_dimension=0, axis_index_groups=rings, tiled=True
    )
    pre_down = lax.ppermute(preact, pair, down)
    pre_across = lax.ppermute(preact, pair, across)
    pre_pair = jnp.concatenate(
        [jnp.where(even, pre_down, pre_across), jnp.where(even, pre_across, preact)]
    ).astype(jnp.float32)
    pre_share = (hidden_share * gelu_slope(pre_pair)).astype(jnp.bfloat16)
    pre_share = lax.ppermute(pre_share, "section", [(1, 0)])
    act_share = gelu_value(pre_pair).astype(jnp.bfloat16)
    right = lax.all_gather(jnp.where(first, pre_share, act_share), "hid", axis=0, tiled=True)

    kept = jnp.where(first, inputs, grad_out)
    given = jnp.where(first, grad_out, inputs)
    taken = lax.ppermute(given, "section", [(0, 1), (1, 0)])
    left_own = jnp.concatenate([jnp.where(first, kept, taken), jnp.where(first, taken, kept)])
    left = jnp.swapaxes(
        spread(left_own, "wid").reshape(wid // 2, 2, 2, rows, features), 1, 2
    ).reshape(2 * wid * rows, features)

    gradient = contract(left, right)
    squares = gradient * gradient
    row_local = jnp.sum(squares, axis=1)
    col_local = jnp.sum(squares, axis=0)
    row_prev = row_state[0]
    col_prev = col_state[0]
    scalars = jnp.stack([jnp.sum(row_local), jnp.sum(row_prev)])
    tail = jnp.concatenate([scalars, jnp.zeros((4 * LANES - 2,), jnp.float32)])
    packed = jnp.concatenate([col_local, tail]).reshape(-1, LANES)
    over_hid = jnp.sum(
        spread(packed, "hid").reshape((hid,) + packed.shape), axis=0
    ).reshape(-1)
    col_total = over_hid[:hidden]
    square_sum, prev_sum = over_hid[hidden], over_hid[hidden + 1]

    partial = lax.dot_general(
        right, own_tile, (((1,), (1,)), ((), ())), preferred_element_type=jnp.float32
    ).astype(jnp.bfloat16)
    blocks = jnp.swapaxes(partial.reshape(wid // 2, 2, 2, rows, features), 1, 2)
    extra = thirds(row_local, square_sum)
    blocks = jnp.concatenate(
        [blocks.reshape(wid, 2 * rows, features), jnp.broadcast_to(extra[None], (wid,) + extra.shape)],
        axis=1,
    )
    over_wid = jnp.sum(exchange(blocks, "wid").astype(jnp.float32), axis=0)
    input_sum = jnp.where(
        first, over_wid[:rows], lax.ppermute(over_wid[rows : 2 * rows], "section", [(0, 1)])
    )
    input_grad = input_sum + grad_out.astype(jnp.float32)
    row_total = jnp.sum(over_wid[2 * rows : 2 * rows + 8], axis=0)
    square_total = jnp.sum(over_wid[2 * rows + 8 :, 0])

    row_moment = decay_rate * row_prev + (1.0 - decay_rate) / FF * row_total
    col_moment = decay_rate * col_prev + (1.0 - decay_rate) / D * col_total
    row_mean = decay_rate / D * prev_sum + (1.0 - decay_rate) / FF / D * square_total
    update = gradient * lax.rsqrt(row_moment[:, None] * col_moment[None, :] / row_mean)
    return (input_grad, update[None])


def solution(mesh):
    placed = (
        P("section", "hid", "wid"),
        P(("section", "hid"), "wid"),
        P(("section", "wid"), "hid"),
        P(("section", "wid"), "hid"),
        P("section", "hid"),
        P("section", "wid"),
    )
    return jax.shard_map(
        shards,
        mesh=mesh,
        in_specs=placed,
        out_specs=(P(("section", "wid"), "hid"), P("section", "hid", "wid")),
        check_vma=False,
    )
```

```python
import jax
import jax.numpy as jnp
from jax import lax
from jax.sharding import PartitionSpec as P

D = 6144
FF = 24576


decay_rate = 0.9
root_half = 0.7071067811865476
inv_root_tau = 0.3989422804014327
LANES = 128


def normal_cdf(pre):
    return 0.5 * (1.0 + lax.erf(pre * root_half))


def gelu_value(pre):
    return pre * normal_cdf(pre)


def gelu_slope(pre):
    return normal_cdf(pre) + pre * jnp.exp(-0.5 * pre * pre) * inv_root_tau


def contract(left, right):
    return lax.dot_general(
        left, right, (((0,), (0,)), ((), ())), preferred_element_type=jnp.float32
    )


def exchange(blocks, axis):
    return lax.all_to_all(blocks, axis, split_axis=0, concat_axis=0, tiled=True)


def spread(block, axis):
    n = lax.axis_size(axis)
    copies = jnp.broadcast_to(block[None], (n,) + block.shape)
    return exchange(copies.reshape((n * block.shape[0],) + block.shape[1:]), axis)


def thirds(values, scalar):
    shape = (16, values.shape[0])
    row = lax.broadcasted_iota(jnp.int32, shape, 0)
    rest = jnp.where(row < 8, jnp.broadcast_to(values[None], shape), scalar)
    out = jnp.zeros(shape, jnp.float32)
    for k in range(3):
        term = lax.reduce_precision(rest, exponent_bits=8, mantissa_bits=7)
        out = jnp.where(row % 8 == k, term, out)
        rest = rest - term
    return out.astype(jnp.bfloat16)


def sum_blocks(partial, axis, groups):
    members = len(groups[0])
    top = jnp.max(jnp.abs(partial), axis=1, keepdims=True)
    power = jnp.clip(jnp.ceil(jnp.log2(jnp.maximum(top, 1e-30))), -96.0, 96.0)
    coded = (partial * jnp.exp2(14.0 - power)).astype(jnp.float16)
    power = jnp.broadcast_to(power, (partial.shape[0], LANES)).astype(jnp.float16)
    coded = jnp.concatenate([coded, power], axis=1).reshape(members, -1, partial.shape[1] + LANES)
    taken = lax.all_to_all(
        coded, axis, split_axis=0, concat_axis=0, axis_index_groups=groups, tiled=True
    )
    power = jnp.max(taken[:, :, -LANES:].astype(jnp.float32), axis=2, keepdims=True)
    return jnp.sum(taken[:, :, :-LANES].astype(jnp.float32) * jnp.exp2(power - 14.0), axis=0)


def shards(weights, preact, inputs, grad_out, row_state, col_state):
    hid = lax.axis_size("hid")
    wid = lax.axis_size("wid")
    own_tile = weights[0]
    features, hidden = own_tile.shape
    rows = grad_out.shape[0]
    first = lax.axis_index("section") == 0
    even = lax.axis_index("hid") % 2 == 0
    pair = ("section", "hid")
    evens = range(0, hid, 2)
    down = [(h, hid + h) for h in evens]
    across = [(h + 1, hid + h) for h in evens] + [(hid + h, hid + h + 1) for h in evens]
    swap = [(hid + h, hid + (h ^ 1)) for h in range(hid)]
    rings = [list(range(p, hid, 2)) for p in range(2)]

    grad_down = lax.ppermute(grad_out, pair, down)
    grad_across = lax.ppermute(grad_out, pair, across)
    next_tile = lax.ppermute(own_tile, pair, swap)
    grad_pair = jnp.concatenate([jnp.where(even, grad_down, grad_out), grad_across], axis=1)
    grad_half = spread(grad_pair, "wid")
    hidden_part = jnp.dot(
        grad_half[:, :features], own_tile, preferred_element_type=jnp.float32
    ) + jnp.dot(grad_half[:, features:], next_tile, preferred_element_type=jnp.float32)
    hidden_share = sum_blocks(hidden_part, "hid", rings)
    pre_down = lax.ppermute(preact, pair, down)
    pre_across = lax.ppermute(preact, pair, across)
    pre_pair = jnp.concatenate(
        [jnp.where(even, pre_down, pre_across), jnp.where(even, pre_across, preact)]
    ).astype(jnp.float32)
    pre_share = (hidden_share * gelu_slope(pre_pair)).astype(jnp.bfloat16)
    pre_share = lax.ppermute(pre_share, "section", [(1, 0)])
    act_share = gelu_value(pre_pair).astype(jnp.bfloat16)
    right = lax.all_gather(jnp.where(first, pre_share, act_share), "hid", axis=0, tiled=True)

    kept = jnp.where(first, inputs, grad_out)
    given = jnp.where(first, grad_out, inputs)
    taken = lax.ppermute(given, "section", [(0, 1), (1, 0)])
    left_own = jnp.concatenate([jnp.where(first, kept, taken), jnp.where(first, taken, kept)])
    left = jnp.swapaxes(
        spread(left_own, "wid").reshape(wid // 2, 2, 2, rows, features), 1, 2
    ).reshape(2 * wid * rows, features)

    gradient = contract(left, right)
    squares = gradient * gradient
    row_local = jnp.sum(squares, axis=1)
    col_local = jnp.sum(squares, axis=0)
    row_prev = row_state[0]
    col_prev = col_state[0]
    scalars = jnp.stack([jnp.sum(row_local), jnp.sum(row_prev)])
    tail = jnp.concatenate([scalars, jnp.zeros((4 * LANES - 2,), jnp.float32)])
    packed = jnp.concatenate([col_local, tail]).reshape(-1, LANES)
    over_hid = jnp.sum(
        spread(packed, "hid").reshape((hid,) + packed.shape), axis=0
    ).reshape(-1)
    col_total = over_hid[:hidden]
    square_sum, prev_sum = over_hid[hidden], over_hid[hidden + 1]

    partial = lax.dot_general(
        right, own_tile, (((1,), (1,)), ((), ())), preferred_element_type=jnp.float32
    ).astype(jnp.bfloat16)
    blocks = jnp.swapaxes(partial.reshape(wid // 2, 2, 2, rows, features), 1, 2)
    extra = thirds(row_local, square_sum)
    blocks = jnp.concatenate(
        [blocks.reshape(wid, 2 * rows, features), jnp.broadcast_to(extra[None], (wid,) + extra.shape)],
        axis=1,
    )
    over_wid = jnp.sum(exchange(blocks, "wid").astype(jnp.float32), axis=0)
    input_sum = jnp.where(
        first, over_wid[:rows], lax.ppermute(over_wid[rows : 2 * rows], "section", [(0, 1)])
    )
    input_grad = input_sum + grad_out.astype(jnp.float32)
    row_total = jnp.sum(over_wid[2 * rows : 2 * rows + 8], axis=0)
    square_total = jnp.sum(over_wid[2 * rows + 8 :, 0])

    row_moment = decay_rate * row_prev + (1.0 - decay_rate) / FF * row_total
    col_moment = decay_rate * col_prev + (1.0 - decay_rate) / D * col_total
    row_mean = decay_rate / D * prev_sum + (1.0 - decay_rate) / FF / D * square_total
    update = gradient * lax.rsqrt(row_moment[:, None] * col_moment[None, :] / row_mean)
    return (input_grad, update[None])


def solution(mesh):
    placed = (
        P("section", "hid", "wid"),
        P(("section", "hid"), "wid"),
        P(("section", "wid"), "hid"),
        P(("section", "wid"), "hid"),
        P("section", "hid"),
        P("section", "wid"),
    )
    return jax.shard_map(
        shards,
        mesh=mesh,
        in_specs=placed,
        out_specs=(P(("section", "wid"), "hid"), P("section", "hid", "wid")),
        check_vma=False,
    )
```

```python
import jax
import jax.numpy as jnp
from jax import lax
from jax.sharding import PartitionSpec as P

D = 6144
FF = 24576


decay_rate = 0.9
root_half = 0.7071067811865476
inv_root_tau = 0.3989422804014327
LANES = 128


def normal_cdf(pre):
    return 0.5 * (1.0 + lax.erf(pre * root_half))


def gelu_value(pre):
    return pre * normal_cdf(pre)


def gelu_slope(pre):
    return normal_cdf(pre) + pre * jnp.exp(-0.5 * pre * pre) * inv_root_tau


def contract(left, right):
    return lax.dot_general(
        left, right, (((0,), (0,)), ((), ())), preferred_element_type=jnp.float32
    )


def exchange(blocks, axis):
    return lax.all_to_all(blocks, axis, split_axis=0, concat_axis=0, tiled=True)


def spread(block, axis):
    n = lax.axis_size(axis)
    copies = jnp.broadcast_to(block[None], (n,) + block.shape)
    return exchange(copies.reshape((n * block.shape[0],) + block.shape[1:]), axis)


def thirds(values, scalar):
    shape = (16, values.shape[0])
    row = lax.broadcasted_iota(jnp.int32, shape, 0)
    rest = jnp.where(row < 8, jnp.broadcast_to(values[None], shape), scalar)
    out = jnp.zeros(shape, jnp.float32)
    for k in range(3):
        term = lax.reduce_precision(rest, exponent_bits=8, mantissa_bits=7)
        out = jnp.where(row % 8 == k, term, out)
        rest = rest - term
    return out.astype(jnp.bfloat16)


def sum_blocks(partial, axis, groups):
    members = len(groups[0])
    columns = partial.shape[1]
    rows = partial.shape[0] // members
    power = jnp.clip(jnp.ceil(jnp.log2(jnp.maximum(jnp.max(jnp.abs(partial)), 1e-30))), -96.0, 96.0)
    coded = (partial * jnp.exp2(14.0 - power)).astype(jnp.float16).reshape(members, rows, columns)
    power = jnp.broadcast_to(power, (members, 8, columns)).astype(jnp.float16)
    taken = lax.all_to_all(
        jnp.concatenate([coded, power], axis=1),
        axis,
        split_axis=0,
        concat_axis=0,
        axis_index_groups=groups,
        tiled=True,
    )
    power = jnp.max(taken[:, rows:, :LANES].astype(jnp.float32), axis=(1, 2), keepdims=True)
    return jnp.sum(taken[:, :rows].astype(jnp.float32) * jnp.exp2(power - 14.0), axis=0)


def shards(weights, preact, inputs, grad_out, row_state, col_state):
    hid = lax.axis_size("hid")
    wid = lax.axis_size("wid")
    own_tile = weights[0]
    features, hidden = own_tile.shape
    half = hidden // 2
    rows = grad_out.shape[0]
    first = lax.axis_index("section") == 0
    even = lax.axis_index("hid") % 2 == 0
    home = lax.axis_index("section") == lax.axis_index("hid") % 2
    pair = ("section", "hid")

    def at(section, h):
        return section * hid + h

    over = [(at(h % 2, h), at(1 - h % 2, h)) for h in range(hid)]
    beside = [(at(h % 2, h ^ 1), at(h % 2, h)) for h in range(hid)]
    across = [(at(h % 2, h ^ 1), at(1 - h % 2, h)) for h in range(hid)]
    rings = [list(range(p, hid, 2)) for p in range(2)]

    def token_blocks(same, other):
        own = jnp.where(home, same, lax.ppermute(other, pair, over))
        near = lax.ppermute(same, pair, beside)
        far = lax.ppermute(other, pair, across)
        return own, jnp.where(home, near, far)

    grad_pair = jnp.concatenate(token_blocks(grad_out, grad_out), axis=1)
    tile_near = lax.ppermute(own_tile[:, :half], pair, [(at(1, h), at(1, h ^ 1)) for h in range(hid)])
    tile_over = lax.ppermute(own_tile[:, half:], pair, [(at(1, h), at(0, h)) for h in range(hid)])
    tile_far = lax.ppermute(own_tile[:, half:], pair, [(at(1, h), at(0, h ^ 1)) for h in range(hid)])
    grad_half = spread(grad_pair, "wid")
    pre_own, pre_next = token_blocks(
        jnp.where(first, preact[:, half:], preact[:, :half]),
        jnp.where(first, preact[:, :half], preact[:, half:]),
    )
    grad_half, pre_own, pre_next = lax.optimization_barrier((grad_half, pre_own, pre_next))
    hidden_part = jnp.dot(
        grad_half[:, :features],
        jnp.where(first, tile_over, own_tile[:, :half]),
        preferred_element_type=jnp.float32,
    ) + jnp.dot(
        grad_half[:, features:],
        jnp.where(first, tile_far, tile_near),
        preferred_element_type=jnp.float32,
    )
    hidden_share = sum_blocks(hidden_part, "hid", rings)
    pre_half = jnp.concatenate(
        [jnp.where(even, pre_own, pre_next), jnp.where(even, pre_next, pre_own)]
    )
    pre_taken = lax.ppermute(pre_half, "section", [(0, 1)])
    act_share = gelu_value(
        jnp.concatenate([pre_half, pre_taken], axis=1).astype(jnp.float32)
    ).astype(jnp.bfloat16)
    pre_share = (hidden_share * gelu_slope(pre_half.astype(jnp.float32))).astype(jnp.bfloat16)
    pre_share = jnp.concatenate(
        [lax.ppermute(pre_share, "section", [(1, 0)]), pre_share], axis=1
    )
    right = lax.all_gather(jnp.where(first, pre_share, act_share), "hid", axis=0, tiled=True)

    kept = jnp.where(first, inputs, grad_out)
    given = jnp.where(first, grad_out, inputs)
    taken = lax.ppermute(given, "section", [(0, 1), (1, 0)])
    left_own = jnp.concatenate([jnp.where(first, kept, taken), jnp.where(first, taken, kept)])
    left = jnp.swapaxes(
        spread(left_own, "wid").reshape(wid // 2, 2, 2, rows, features), 1, 2
    ).reshape(2 * wid * rows, features)

    gradient = contract(left, right)
    squares = gradient * gradient
    row_local = jnp.sum(squares, axis=1)
    col_local = jnp.sum(squares, axis=0)
    row_prev = row_state[0]
    col_prev = col_state[0]
    scalars = jnp.stack([jnp.sum(row_local), jnp.sum(row_prev)])
    tail = jnp.concatenate([scalars, jnp.zeros((4 * LANES - 2,), jnp.float32)])
    packed = jnp.concatenate([col_local, tail]).reshape(-1, LANES)
    over_hid = jnp.sum(
        spread(packed, "hid").reshape((hid,) + packed.shape), axis=0
    ).reshape(-1)
    col_total = over_hid[:hidden]
    square_sum, prev_sum = over_hid[hidden], over_hid[hidden + 1]

    partial = lax.dot_general(
        right, own_tile, (((1,), (1,)), ((), ())), preferred_element_type=jnp.float32
    ).astype(jnp.bfloat16)
    blocks = jnp.swapaxes(partial.reshape(wid // 2, 2, 2, rows, features), 1, 2)
    extra = thirds(row_local, square_sum)
    blocks = jnp.concatenate(
        [blocks.reshape(wid, 2 * rows, features), jnp.broadcast_to(extra[None], (wid,) + extra.shape)],
        axis=1,
    )
    over_wid = jnp.sum(exchange(blocks, "wid").astype(jnp.float32), axis=0)
    input_sum = jnp.where(
        first, over_wid[:rows], lax.ppermute(over_wid[rows : 2 * rows], "section", [(0, 1)])
    )
    input_grad = input_sum + grad_out.astype(jnp.float32)
    row_total = jnp.sum(over_wid[2 * rows : 2 * rows + 8], axis=0)
    square_total = jnp.sum(over_wid[2 * rows + 8 :, 0])

    row_moment = decay_rate * row_prev + (1.0 - decay_rate) / FF * row_total
    col_moment = decay_rate * col_prev + (1.0 - decay_rate) / D * col_total
    row_mean = decay_rate / D * prev_sum + (1.0 - decay_rate) / FF / D * square_total
    update = gradient * lax.rsqrt(row_moment[:, None] * col_moment[None, :] / row_mean)
    return (input_grad, update[None])


def solution(mesh):
    placed = (
        P("section", "hid", "wid"),
        P(("section", "hid"), "wid"),
        P(("section", "wid"), "hid"),
        P(("section", "wid"), "hid"),
        P("section", "hid"),
        P("section", "wid"),
    )
    return jax.shard_map(
        shards,
        mesh=mesh,
        in_specs=placed,
        out_specs=(P(("section", "wid"), "hid"), P("section", "hid", "wid")),
        check_vma=False,
    )
```

```python
import jax
import jax.numpy as jnp
from jax import lax
from jax.experimental.layout import Layout, with_layout_constraint
from jax.sharding import PartitionSpec as P


D = 6144
FF = 24576


decay_rate = 0.9
root_half = 0.7071067811865476
inv_root_tau = 0.3989422804014327
LANES = 128


def normal_cdf(pre):
    return 0.5 * (1.0 + lax.erf(pre * root_half))


def gelu_value(pre):
    return pre * normal_cdf(pre)


def gelu_slope(pre):
    return normal_cdf(pre) + pre * jnp.exp(-0.5 * pre * pre) * inv_root_tau


def by_rows(block):
    return with_layout_constraint(block, Layout(major_to_minor=(0, 1)))


def contract(left, right):
    return lax.dot_general(
        left, right, (((0,), (0,)), ((), ())), preferred_element_type=jnp.float32
    )


def exchange(blocks, axis):
    return lax.all_to_all(blocks, axis, split_axis=0, concat_axis=0, tiled=True)


def spread(block, axis):
    n = lax.axis_size(axis)
    copies = jnp.broadcast_to(block[None], (n,) + block.shape)
    return exchange(copies.reshape((n * block.shape[0],) + block.shape[1:]), axis)


def thirds(values, scalar):
    shape = (8, 2 * values.shape[0])
    row = lax.broadcasted_iota(jnp.int32, shape, 0)
    rest = jnp.concatenate([values, jnp.broadcast_to(scalar, values.shape)])
    rest = jnp.broadcast_to(rest[None], shape)
    out = jnp.zeros(shape, jnp.float32)
    for k in range(3):
        term = lax.reduce_precision(rest, exponent_bits=8, mantissa_bits=7)
        out = jnp.where(row == k, term, out)
        rest = rest - term
    return out.astype(jnp.bfloat16)


def sum_blocks(partial, axis, groups):
    members = len(groups[0])
    columns = partial.shape[1]
    rows = partial.shape[0] // members
    power = jnp.clip(jnp.ceil(jnp.log2(jnp.maximum(jnp.max(jnp.abs(partial)), 1e-30))), -96.0, 96.0)
    coded = (partial * jnp.exp2(14.0 - power)).astype(jnp.float16).reshape(members, rows, columns)
    power = jnp.broadcast_to(power, (members, 8, columns)).astype(jnp.float16)
    taken = lax.all_to_all(
        jnp.concatenate([coded, power], axis=1),
        axis,
        split_axis=0,
        concat_axis=0,
        axis_index_groups=groups,
        tiled=True,
    )
    power = jnp.max(taken[:, rows:, :LANES].astype(jnp.float32), axis=(1, 2), keepdims=True)
    return jnp.sum(taken[:, :rows].astype(jnp.float32) * jnp.exp2(power - 14.0), axis=0)


def shards(weights, preact, inputs, grad_out, row_state, col_state):
    hid = lax.axis_size("hid")
    wid = lax.axis_size("wid")
    own_tile = weights[0]
    features, hidden = own_tile.shape
    half = hidden // 2
    rows = grad_out.shape[0]
    first = lax.axis_index("section") == 0
    even = lax.axis_index("hid") % 2 == 0
    home = lax.axis_index("section") == lax.axis_index("hid") % 2
    pair = ("section", "hid")

    def at(section, h):
        return section * hid + h

    over = [(at(h % 2, h), at(1 - h % 2, h)) for h in range(hid)]
    beside = [(at(h % 2, h ^ 1), at(h % 2, h)) for h in range(hid)]
    across = [(at(h % 2, h ^ 1), at(1 - h % 2, h)) for h in range(hid)]
    rings = [list(range(p, hid, 2)) for p in range(2)]

    def token_blocks(same, other):
        same, other = lax.optimization_barrier((same, other))
        far = lax.ppermute(other, pair, across)
        return same, lax.ppermute(other, pair, over), lax.ppermute(same, pair, beside), far

    def pick(blocks, columns):
        same, there, near, far = (block[:, columns] for block in blocks)
        return jnp.where(home, same, there), jnp.where(home, near, far)

    tile_near = lax.ppermute(
        by_rows(jnp.where(first & even, own_tile[:, half:], own_tile[:, :half])),
        "hid",
        [(h, h ^ 1) for h in range(hid)],
    )
    tile_over = lax.ppermute(own_tile[:, half:], pair, [(at(1, h), at(0, h)) for h in range(hid)])
    tile_far = lax.ppermute(
        own_tile[:, half:], pair, [(at(1, h), at(0, h ^ 1)) for h in range(hid)]
    )
    blocks = token_blocks(
        jnp.concatenate([grad_out, jnp.where(first, preact[:, half:], preact[:, :half])], axis=1),
        jnp.concatenate([grad_out, jnp.where(first, preact[:, :half], preact[:, half:])], axis=1),
    )
    grad_half = spread(jnp.concatenate(pick(blocks, slice(features)), axis=1), "wid")
    hidden_part = jnp.dot(
        grad_half[:, :features],
        jnp.where(first, tile_over, own_tile[:, :half]),
        preferred_element_type=jnp.float32,
    ) + jnp.dot(
        grad_half[:, features:],
        jnp.where(first, tile_far, tile_near),
        preferred_element_type=jnp.float32,
    )
    hidden_share = sum_blocks(hidden_part, "hid", rings)
    pre_own, pre_next = pick(blocks, slice(features, None))
    pre_half = jnp.concatenate(
        [jnp.where(even, pre_own, pre_next), jnp.where(even, pre_next, pre_own)]
    )

    def column_blocks(own, near):
        return jnp.concatenate([jnp.where(even, own, near), jnp.where(even, near, own)])

    evens = range(0, hid, 2)
    pre_over = lax.ppermute(pre_half, pair, [(at(0, h + 1), at(1, h + 1)) for h in evens])
    pre_near = lax.ppermute(
        pre_half,
        pair,
        [(at(1, h + 1), at(1, h)) for h in evens] + [(at(0, h), at(1, h + 1)) for h in evens],
    )
    act_share = gelu_value(
        column_blocks(jnp.where(even, pre_half, pre_over), pre_near).astype(jnp.float32)
    ).astype(jnp.bfloat16)
    pre_share = (hidden_share * gelu_slope(pre_half.astype(jnp.float32))).astype(jnp.bfloat16)
    share_over = lax.ppermute(pre_share, pair, [(at(1, h), at(0, h)) for h in evens])
    share_near = lax.ppermute(
        pre_share,
        pair,
        [(at(1, h + 1), at(0, h)) for h in evens] + [(at(0, h), at(0, h + 1)) for h in evens],
    )
    pre_share = column_blocks(jnp.where(even, share_over, pre_share), share_near)
    right = lax.all_gather(
        jnp.where(first, pre_share, act_share), "hid", axis=0, axis_index_groups=rings, tiled=True
    )

    def neighbour(block):
        return lax.ppermute(block, "hid", [(h, h ^ 1) for h in range(hid)])

    kept = jnp.where(first, inputs, grad_out)
    given = jnp.where(first, grad_out, inputs)
    taken = lax.ppermute(given, "section", [(0, 1), (1, 0)])
    left_own = jnp.concatenate([jnp.where(first, kept, taken), jnp.where(first, taken, kept)])
    left = spread(jnp.concatenate([left_own, neighbour(left_own)], axis=1), "wid")
    left = jnp.swapaxes(left.reshape(wid // 2, 2, 2, rows, 2 * features), 1, 2)
    left = left.reshape(2 * wid * rows, 2 * features)

    both = by_rows(contract(left, right))
    squares = both * both
    row_both = jnp.sum(squares, axis=1)
    col_local = jnp.sum(squares, axis=0)
    swapped = neighbour(both[features:])
    row_prev = row_state[0]
    col_prev = col_state[0]
    scalars = jnp.stack([jnp.sum(row_both), jnp.sum(row_prev)])
    packed = jnp.concatenate(
        [col_local, row_both[features:], scalars, jnp.zeros((-(half + features + 2) % (8 * LANES),), jnp.float32)]
    ).reshape(-1, LANES)
    taken = spread(packed, "hid").reshape((hid,) + packed.shape)
    over_hid = jnp.sum(taken.reshape((hid // 2, 2) + packed.shape), axis=0).reshape(2, -1)
    col_total = over_hid[:, :half].reshape(-1)
    square_sum = over_hid[0, half + features] + over_hid[1, half + features]
    prev_sum = over_hid[0, half + features + 1] + over_hid[1, half + features + 1]
    is_near = lax.broadcasted_iota(jnp.int32, (hid, 1, 1), 0) == lax.axis_index("hid") ^ 1
    row_near = jnp.sum(
        jnp.where(is_near, taken[:, half // LANES : (half + features) // LANES], 0.0), axis=0
    ).reshape(-1)
    row_local = row_both[:features] + row_near

    my_columns = jnp.where(even, own_tile[:, :half], own_tile[:, half:])
    my_columns, tile_next = lax.optimization_barrier((by_rows(my_columns), by_rows(tile_near)))

    def input_blocks(tile):
        partial = lax.dot_general(
            right, tile, (((1,), (1,)), ((), ())), preferred_element_type=jnp.float32
        ).astype(jnp.bfloat16)
        blocks = jnp.swapaxes(partial.reshape(wid // 2, 2, 2, rows, features), 1, 2)
        return blocks.reshape(wid, 2 * rows, features)

    blocks = jnp.concatenate([input_blocks(my_columns), input_blocks(tile_next)], axis=2)
    extra = thirds(row_local, square_sum)
    blocks = jnp.concatenate([blocks, jnp.broadcast_to(extra[None], (wid,) + extra.shape)], axis=1)
    over_wid = jnp.sum(exchange(blocks, "wid").astype(jnp.float32), axis=0)
    mine, others = over_wid[: 2 * rows, :features], over_wid[: 2 * rows, features:]
    near_sum = lax.ppermute(others[:rows], pair, [(at(0, h), at(0, h ^ 1)) for h in range(hid)])
    over_sum = lax.ppermute(mine[rows:], pair, [(at(0, h), at(1, h)) for h in range(hid)])
    far_sum = lax.ppermute(others[rows:], pair, [(at(0, h), at(1, h ^ 1)) for h in range(hid)])
    input_sum = jnp.where(first, mine[:rows], over_sum) + jnp.where(first, near_sum, far_sum)
    input_grad = input_sum + grad_out.astype(jnp.float32)
    totals = jnp.sum(over_wid[2 * rows :], axis=0)
    row_total, square_total = totals[:features], totals[features]

    own_half = both[:features]
    gradient = jnp.concatenate(
        [jnp.where(even, own_half, swapped), jnp.where(even, swapped, own_half)], axis=1
    )
    row_moment = decay_rate * row_prev + (1.0 - decay_rate) / FF * row_total
    col_moment = decay_rate * col_prev + (1.0 - decay_rate) / D * col_total
    row_mean = decay_rate / D * prev_sum + (1.0 - decay_rate) / FF / D * square_total
    update = gradient * lax.rsqrt(row_moment[:, None] * col_moment[None, :] / row_mean)
    return (input_grad, update[None])


def solution(mesh):
    placed = (
        P("section", "hid", "wid"),
        P(("section", "hid"), "wid"),
        P(("section", "wid"), "hid"),
        P(("section", "wid"), "hid"),
        P("section", "hid"),
        P("section", "wid"),
    )

    return jax.shard_map(
        shards,
        mesh=mesh,
        in_specs=placed,
        out_specs=(P(("section", "wid"), "hid"), P("section", "hid", "wid")),
        check_vma=False,
    )
```

```python
import jax
import jax.numpy as jnp
from jax import lax
from jax.experimental.layout import Layout, with_layout_constraint
from jax.sharding import PartitionSpec as P


D = 6144
FF = 24576


decay_rate = 0.9
root_half = 0.7071067811865476
inv_root_tau = 0.3989422804014327
LANES = 128


def normal_cdf(pre):
    return 0.5 * (1.0 + lax.erf(pre * root_half))


def gelu_value(pre):
    return pre * normal_cdf(pre)


def gelu_slope(pre):
    return normal_cdf(pre) + pre * jnp.exp(-0.5 * pre * pre) * inv_root_tau


def by_rows(block):
    return with_layout_constraint(block, Layout(major_to_minor=(0, 1)))


def contract(left, right):
    return lax.dot_general(
        left, right, (((0,), (0,)), ((), ())), preferred_element_type=jnp.float32
    )


def exchange(blocks, axis):
    return lax.all_to_all(blocks, axis, split_axis=0, concat_axis=0, tiled=True)


def spread(block, axis):
    n = lax.axis_size(axis)
    copies = jnp.broadcast_to(block[None], (n,) + block.shape)
    return exchange(copies.reshape((n * block.shape[0],) + block.shape[1:]), axis)


def thirds(values, scalar):
    shape = (8, 2 * values.shape[0])
    row = lax.broadcasted_iota(jnp.int32, shape, 0)
    rest = jnp.concatenate([values, jnp.broadcast_to(scalar, values.shape)])
    rest = jnp.broadcast_to(rest[None], shape)
    out = jnp.zeros(shape, jnp.float32)
    for k in range(3):
        term = lax.reduce_precision(rest, exponent_bits=8, mantissa_bits=7)
        out = jnp.where(row == k, term, out)
        rest = rest - term
    return out.astype(jnp.bfloat16)


def sum_blocks(partial, axis, groups):
    members = len(groups[0])
    columns = partial.shape[1]
    rows = partial.shape[0] // members
    power = jnp.clip(jnp.ceil(jnp.log2(jnp.maximum(jnp.max(jnp.abs(partial)), 1e-30))), -96.0, 96.0)
    coded = (partial * jnp.exp2(14.0 - power)).astype(jnp.float16).reshape(members, rows, columns)
    power = jnp.broadcast_to(power, (members, 8, columns)).astype(jnp.float16)
    taken = lax.all_to_all(
        jnp.concatenate([coded, power], axis=1),
        axis,
        split_axis=0,
        concat_axis=0,
        axis_index_groups=groups,
        tiled=True,
    )
    power = jnp.max(taken[:, rows:, :LANES].astype(jnp.float32), axis=(1, 2), keepdims=True)
    return jnp.sum(taken[:, :rows].astype(jnp.float32) * jnp.exp2(power - 14.0), axis=0)


def shards(weights, preact, inputs, grad_out, row_state, col_state):
    hid = lax.axis_size("hid")
    wid = lax.axis_size("wid")
    own_tile = weights[0]
    features, hidden = own_tile.shape
    half = hidden // 2
    rows = grad_out.shape[0]
    first = lax.axis_index("section") == 0
    even = lax.axis_index("hid") % 2 == 0
    home = lax.axis_index("section") == lax.axis_index("hid") % 2
    pair = ("section", "hid")

    def at(section, h):
        return section * hid + h

    over = [(at(h % 2, h), at(1 - h % 2, h)) for h in range(hid)]
    beside = [(at(h % 2, h ^ 1), at(h % 2, h)) for h in range(hid)]
    across = [(at(h % 2, h ^ 1), at(1 - h % 2, h)) for h in range(hid)]
    rings = [list(range(p, hid, 2)) for p in range(2)]

    def token_blocks(same, other):
        same, other = lax.optimization_barrier((same, other))
        far = lax.ppermute(other, pair, across)
        return same, lax.ppermute(other, pair, over), lax.ppermute(same, pair, beside), far

    def pick(blocks):
        same, there, near, far = blocks
        return jnp.where(home, same, there), jnp.where(home, near, far)

    grad_blocks = token_blocks(grad_out, grad_out)
    tile_near = lax.ppermute(
        by_rows(jnp.where(first & even, own_tile[:, half:], own_tile[:, :half])),
        "hid",
        [(h, h ^ 1) for h in range(hid)],
    )
    tile_over = lax.ppermute(own_tile[:, half:], pair, [(at(1, h), at(0, h)) for h in range(hid)])
    tile_far = lax.ppermute(
        own_tile[:, half:], pair, [(at(1, h), at(0, h ^ 1)) for h in range(hid)]
    )
    pre_blocks = token_blocks(
        jnp.where(first, preact[:, half:], preact[:, :half]),
        jnp.where(first, preact[:, :half], preact[:, half:]),
    )
    grad_half = spread(jnp.concatenate(pick(grad_blocks), axis=1), "wid")
    hidden_part = jnp.dot(
        grad_half[:, :features],
        jnp.where(first, tile_over, own_tile[:, :half]),
        preferred_element_type=jnp.float32,
    ) + jnp.dot(
        grad_half[:, features:],
        jnp.where(first, tile_far, tile_near),
        preferred_element_type=jnp.float32,
    )
    hidden_share = sum_blocks(hidden_part, "hid", rings)
    pre_own, pre_next = pick(pre_blocks)
    pre_half = jnp.concatenate(
        [jnp.where(even, pre_own, pre_next), jnp.where(even, pre_next, pre_own)]
    )

    def column_blocks(own, near):
        return jnp.concatenate([jnp.where(even, own, near), jnp.where(even, near, own)])

    evens = range(0, hid, 2)
    pre_over = lax.ppermute(pre_half, pair, [(at(0, h + 1), at(1, h + 1)) for h in evens])
    pre_near = lax.ppermute(
        pre_half,
        pair,
        [(at(1, h + 1), at(1, h)) for h in evens] + [(at(0, h), at(1, h + 1)) for h in evens],
    )
    act_share = gelu_value(
        column_blocks(jnp.where(even, pre_half, pre_over), pre_near).astype(jnp.float32)
    ).astype(jnp.bfloat16)
    pre_share = (hidden_share * gelu_slope(pre_half.astype(jnp.float32))).astype(jnp.bfloat16)
    share_over = lax.ppermute(pre_share, pair, [(at(1, h), at(0, h)) for h in evens])
    share_near = lax.ppermute(
        pre_share,
        pair,
        [(at(1, h + 1), at(0, h)) for h in evens] + [(at(0, h), at(0, h + 1)) for h in evens],
    )
    pre_share = column_blocks(jnp.where(even, share_over, pre_share), share_near)
    right = lax.all_gather(
        jnp.where(first, pre_share, act_share), "hid", axis=0, axis_index_groups=rings, tiled=True
    )

    def neighbour(block):
        return lax.ppermute(block, "hid", [(h, h ^ 1) for h in range(hid)])

    kept = jnp.where(first, inputs, grad_out)
    given = jnp.where(first, grad_out, inputs)
    taken = lax.ppermute(given, "section", [(0, 1), (1, 0)])
    left_own = jnp.concatenate([jnp.where(first, kept, taken), jnp.where(first, taken, kept)])
    left = spread(jnp.concatenate([left_own, neighbour(left_own)], axis=1), "wid")
    left = jnp.swapaxes(left.reshape(wid // 2, 2, 2, rows, 2 * features), 1, 2)
    left = left.reshape(2 * wid * rows, 2 * features)

    both = by_rows(contract(left, right))
    squares = both * both
    row_both = jnp.sum(squares, axis=1)
    col_local = jnp.sum(squares, axis=0)
    swapped = neighbour(both[features:])
    row_prev = row_state[0]
    col_prev = col_state[0]
    scalars = jnp.stack([jnp.sum(row_both), jnp.sum(row_prev)])
    packed = jnp.concatenate(
        [col_local, row_both[features:], scalars, jnp.zeros((-(half + features + 2) % (8 * LANES),), jnp.float32)]
    ).reshape(-1, LANES)
    taken = spread(packed, "hid").reshape((hid,) + packed.shape)
    over_hid = jnp.sum(taken.reshape((hid // 2, 2) + packed.shape), axis=0).reshape(2, -1)
    col_total = over_hid[:, :half].reshape(-1)
    square_sum = over_hid[0, half + features] + over_hid[1, half + features]
    prev_sum = over_hid[0, half + features + 1] + over_hid[1, half + features + 1]
    is_near = lax.broadcasted_iota(jnp.int32, (hid, 1, 1), 0) == lax.axis_index("hid") ^ 1
    row_near = jnp.sum(
        jnp.where(is_near, taken[:, half // LANES : (half + features) // LANES], 0.0), axis=0
    ).reshape(-1)
    row_local = row_both[:features] + row_near

    my_columns = jnp.where(even, own_tile[:, :half], own_tile[:, half:])
    my_columns, tile_next = lax.optimization_barrier((by_rows(my_columns), by_rows(tile_near)))

    def input_blocks(tile):
        partial = lax.dot_general(
            right, tile, (((1,), (1,)), ((), ())), preferred_element_type=jnp.float32
        ).astype(jnp.bfloat16)
        blocks = jnp.swapaxes(partial.reshape(wid // 2, 2, 2, rows, features), 1, 2)
        return blocks.reshape(wid, 2 * rows, features)

    blocks = jnp.concatenate([input_blocks(my_columns), input_blocks(tile_next)], axis=2)
    extra = thirds(row_local, square_sum)
    blocks = jnp.concatenate([blocks, jnp.broadcast_to(extra[None], (wid,) + extra.shape)], axis=1)
    over_wid = jnp.sum(exchange(blocks, "wid").astype(jnp.float32), axis=0)
    mine, others = over_wid[: 2 * rows, :features], over_wid[: 2 * rows, features:]
    near_sum = lax.ppermute(others[:rows], pair, [(at(0, h), at(0, h ^ 1)) for h in range(hid)])
    over_sum = lax.ppermute(mine[rows:], pair, [(at(0, h), at(1, h)) for h in range(hid)])
    far_sum = lax.ppermute(others[rows:], pair, [(at(0, h), at(1, h ^ 1)) for h in range(hid)])
    input_sum = jnp.where(first, mine[:rows], over_sum) + jnp.where(first, near_sum, far_sum)
    input_grad = input_sum + grad_out.astype(jnp.float32)
    totals = jnp.sum(over_wid[2 * rows :], axis=0)
    row_total, square_total = totals[:features], totals[features]

    own_half = both[:features]
    gradient = jnp.concatenate(
        [jnp.where(even, own_half, swapped), jnp.where(even, swapped, own_half)], axis=1
    )
    row_moment = decay_rate * row_prev + (1.0 - decay_rate) / FF * row_total
    col_moment = decay_rate * col_prev + (1.0 - decay_rate) / D * col_total
    row_mean = decay_rate / D * prev_sum + (1.0 - decay_rate) / FF / D * square_total
    update = gradient * lax.rsqrt(row_moment[:, None] * col_moment[None, :] / row_mean)
    return (input_grad, update[None])


def solution(mesh):
    placed = (
        P("section", "hid", "wid"),
        P(("section", "hid"), "wid"),
        P(("section", "wid"), "hid"),
        P(("section", "wid"), "hid"),
        P("section", "hid"),
        P("section", "wid"),
    )

    return jax.shard_map(
        shards,
        mesh=mesh,
        in_specs=placed,
        out_specs=(P(("section", "wid"), "hid"), P("section", "hid", "wid")),
        check_vma=False,
    )
```

```python
import jax
import jax.numpy as jnp
from jax import lax
from jax.experimental.layout import Layout, with_layout_constraint
from jax.sharding import PartitionSpec as P


D = 6144
FF = 24576


decay_rate = 0.9
root_half = 0.7071067811865476
inv_root_tau = 0.3989422804014327
LANES = 128


def normal_cdf(pre):
    return 0.5 * (1.0 + lax.erf(pre * root_half))


def gelu_value(pre):
    return pre * normal_cdf(pre)


def gelu_slope(pre):
    return normal_cdf(pre) + pre * jnp.exp(-0.5 * pre * pre) * inv_root_tau


def by_rows(block):
    return with_layout_constraint(block, Layout(major_to_minor=(0, 1)))


def contract(left, right):
    return lax.dot_general(
        left, right, (((0,), (0,)), ((), ())), preferred_element_type=jnp.float32
    )


def exchange(blocks, axis):
    return lax.all_to_all(blocks, axis, split_axis=0, concat_axis=0, tiled=True)


def spread(block, axis):
    n = lax.axis_size(axis)
    copies = jnp.broadcast_to(block[None], (n,) + block.shape)
    return exchange(copies.reshape((n * block.shape[0],) + block.shape[1:]), axis)


def thirds(values, scalar):
    shape = (8, 2 * values.shape[0])
    row = lax.broadcasted_iota(jnp.int32, shape, 0)
    rest = jnp.concatenate([values, jnp.broadcast_to(scalar, values.shape)])
    rest = jnp.broadcast_to(rest[None], shape)
    out = jnp.zeros(shape, jnp.float32)
    for k in range(3):
        term = lax.reduce_precision(rest, exponent_bits=8, mantissa_bits=7)
        out = jnp.where(row == k, term, out)
        rest = rest - term
    return out.astype(jnp.bfloat16)


def scale_power(top):
    return jnp.clip(jnp.ceil(jnp.log2(jnp.maximum(top, 1e-30))), -96.0, 96.0)


def sum_blocks(partial, axis, groups):
    members = len(groups[0])
    columns = partial.shape[1]
    rows = partial.shape[0] // members
    power = scale_power(jnp.max(jnp.abs(partial)))
    coded = (partial * jnp.exp2(14.0 - power)).astype(jnp.float16).reshape(members, rows, columns)
    power = jnp.broadcast_to(power, (members, 8, columns)).astype(jnp.float16)
    taken = lax.all_to_all(
        jnp.concatenate([coded, power], axis=1),
        axis,
        split_axis=0,
        concat_axis=0,
        axis_index_groups=groups,
        tiled=True,
    )
    power = jnp.max(taken[:, rows:, :LANES].astype(jnp.float32), axis=(1, 2), keepdims=True)
    return jnp.sum(taken[:, :rows].astype(jnp.float32) * jnp.exp2(power - 14.0), axis=0)


def shards(weights, preact, inputs, grad_out, row_state, col_state):
    hid = lax.axis_size("hid")
    wid = lax.axis_size("wid")
    own_tile = weights[0]
    features, hidden = own_tile.shape
    half = hidden // 2
    rows = grad_out.shape[0]
    first = lax.axis_index("section") == 0
    even = lax.axis_index("hid") % 2 == 0
    home = lax.axis_index("section") == lax.axis_index("hid") % 2
    pair = ("section", "hid")

    def at(section, h):
        return section * hid + h

    over = [(at(h % 2, h), at(1 - h % 2, h)) for h in range(hid)]
    beside = [(at(h % 2, h ^ 1), at(h % 2, h)) for h in range(hid)]
    across = [(at(h % 2, h ^ 1), at(1 - h % 2, h)) for h in range(hid)]
    rings = [list(range(p, hid, 2)) for p in range(2)]

    def token_blocks(same, other):
        same, other = lax.optimization_barrier((same, other))
        far = lax.ppermute(other, pair, across)
        return same, lax.ppermute(other, pair, over), lax.ppermute(same, pair, beside), far

    def pick(blocks):
        same, there, near, far = blocks
        return jnp.where(home, same, there), jnp.where(home, near, far)

    grad_blocks = token_blocks(grad_out, grad_out)
    tile_near = lax.ppermute(
        by_rows(jnp.where(first & even, own_tile[:, half:], own_tile[:, :half])),
        "hid",
        [(h, h ^ 1) for h in range(hid)],
    )
    tile_over = lax.ppermute(own_tile[:, half:], pair, [(at(1, h), at(0, h)) for h in range(hid)])
    tile_far = lax.ppermute(
        own_tile[:, half:], pair, [(at(1, h), at(0, h ^ 1)) for h in range(hid)]
    )
    pre_blocks = token_blocks(
        jnp.where(first, preact[:, half:], preact[:, :half]),
        jnp.where(first, preact[:, :half], preact[:, half:]),
    )
    grad_half = spread(jnp.concatenate(pick(grad_blocks), axis=1), "wid")
    hidden_part = jnp.dot(
        grad_half[:, :features],
        jnp.where(first, tile_over, own_tile[:, :half]),
        preferred_element_type=jnp.float32,
    ) + jnp.dot(
        grad_half[:, features:],
        jnp.where(first, tile_far, tile_near),
        preferred_element_type=jnp.float32,
    )
    hidden_share = sum_blocks(hidden_part, "hid", rings)
    pre_own, pre_next = pick(pre_blocks)
    pre_half = jnp.concatenate(
        [jnp.where(even, pre_own, pre_next), jnp.where(even, pre_next, pre_own)]
    )

    def column_blocks(own, near):
        return jnp.concatenate([jnp.where(even, own, near), jnp.where(even, near, own)])

    evens = range(0, hid, 2)
    pre_over = lax.ppermute(pre_half, pair, [(at(0, h + 1), at(1, h + 1)) for h in evens])
    pre_near = lax.ppermute(
        pre_half,
        pair,
        [(at(1, h + 1), at(1, h)) for h in evens] + [(at(0, h), at(1, h + 1)) for h in evens],
    )
    act_share = gelu_value(
        column_blocks(jnp.where(even, pre_half, pre_over), pre_near).astype(jnp.float32)
    ).astype(jnp.bfloat16)
    pre_share = (hidden_share * gelu_slope(pre_half.astype(jnp.float32))).astype(jnp.bfloat16)
    share_over = lax.ppermute(pre_share, pair, [(at(1, h), at(0, h)) for h in evens])
    share_near = lax.ppermute(
        pre_share,
        pair,
        [(at(1, h + 1), at(0, h)) for h in evens] + [(at(0, h), at(0, h + 1)) for h in evens],
    )
    pre_share = column_blocks(jnp.where(even, share_over, pre_share), share_near)
    right = lax.all_gather(
        jnp.where(first, pre_share, act_share), "hid", axis=0, axis_index_groups=rings, tiled=True
    )

    def neighbour(block):
        return lax.ppermute(block, "hid", [(h, h ^ 1) for h in range(hid)])

    kept = jnp.where(first, inputs, grad_out)
    given = jnp.where(first, grad_out, inputs)
    taken = lax.ppermute(given, "section", [(0, 1), (1, 0)])
    left_own = jnp.concatenate([jnp.where(first, kept, taken), jnp.where(first, taken, kept)])
    left = spread(jnp.concatenate([left_own, neighbour(left_own)], axis=1), "wid")
    left = jnp.swapaxes(left.reshape(wid // 2, 2, 2, rows, 2 * features), 1, 2)
    left = left.reshape(2 * wid * rows, 2 * features)

    both = by_rows(contract(left, right))
    squares = both * both
    row_both = jnp.sum(squares, axis=1)
    col_local = jnp.sum(squares, axis=0)
    power = scale_power(jnp.sqrt(jnp.sum(row_both[features:])))
    swapped = neighbour((both[features:] * jnp.exp2(14.0 - power)).astype(jnp.float16))
    row_prev = row_state[0]
    col_prev = col_state[0]
    scalars = jnp.stack([jnp.sum(row_both), jnp.sum(row_prev), power])
    packed = jnp.concatenate(
        [col_local, row_both[features:], scalars, jnp.zeros((-(half + features + 3) % (8 * LANES),), jnp.float32)]
    ).reshape(-1, LANES)
    taken = spread(packed, "hid").reshape((hid,) + packed.shape)
    over_hid = jnp.sum(taken.reshape((hid // 2, 2) + packed.shape), axis=0).reshape(2, -1)
    col_total = over_hid[:, :half].reshape(-1)
    square_sum = over_hid[0, half + features] + over_hid[1, half + features]
    prev_sum = over_hid[0, half + features + 1] + over_hid[1, half + features + 1]
    is_near = lax.broadcasted_iota(jnp.int32, (hid, 1, 1), 0) == lax.axis_index("hid") ^ 1
    from_near = jnp.sum(
        jnp.where(is_near, taken[:, half // LANES : (half + features) // LANES + 1], 0.0), axis=0
    ).reshape(-1)
    row_local = row_both[:features] + from_near[:features]
    power_near = from_near[features + 2]

    my_columns = jnp.where(even, own_tile[:, :half], own_tile[:, half:])
    my_columns, tile_next = lax.optimization_barrier((by_rows(my_columns), by_rows(tile_near)))

    def input_blocks(tile):
        partial = lax.dot_general(
            right, tile, (((1,), (1,)), ((), ())), preferred_element_type=jnp.float32
        ).astype(jnp.bfloat16)
        blocks = jnp.swapaxes(partial.reshape(wid // 2, 2, 2, rows, features), 1, 2)
        return blocks.reshape(wid, 2 * rows, features)

    blocks = jnp.concatenate([input_blocks(my_columns), input_blocks(tile_next)], axis=2)
    extra = thirds(row_local, square_sum)
    blocks = jnp.concatenate([blocks, jnp.broadcast_to(extra[None], (wid,) + extra.shape)], axis=1)
    blocks = exchange(blocks, "wid")
    over_wid = jnp.sum(blocks.astype(jnp.float32), axis=0)
    mine, others = over_wid[: 2 * rows, :features], over_wid[: 2 * rows, features:]
    near_sum = lax.ppermute(others[:rows], pair, [(at(0, h), at(0, h ^ 1)) for h in range(hid)])
    over_sum = lax.ppermute(mine[rows:], pair, [(at(0, h), at(1, h)) for h in range(hid)])
    far_sum = lax.ppermute(others[rows:], pair, [(at(0, h), at(1, h ^ 1)) for h in range(hid)])
    input_sum = jnp.where(first, mine[:rows], over_sum) + jnp.where(first, near_sum, far_sum)
    input_grad = input_sum + grad_out.astype(jnp.float32)
    totals = jnp.sum(over_wid[2 * rows :], axis=0)
    row_total, square_total = totals[:features], totals[features]

    own_half = both[:features]
    swapped = swapped.astype(jnp.float32) * jnp.exp2(power_near - 14.0)
    gradient = jnp.concatenate(
        [jnp.where(even, own_half, swapped), jnp.where(even, swapped, own_half)], axis=1
    )
    row_moment = decay_rate * row_prev + (1.0 - decay_rate) / FF * row_total
    col_moment = decay_rate * col_prev + (1.0 - decay_rate) / D * col_total
    row_mean = decay_rate / D * prev_sum + (1.0 - decay_rate) / FF / D * square_total
    update = gradient * lax.rsqrt(row_moment[:, None] * col_moment[None, :] / row_mean)
    return (input_grad, update[None])


def solution(mesh):
    placed = (
        P("section", "hid", "wid"),
        P(("section", "hid"), "wid"),
        P(("section", "wid"), "hid"),
        P(("section", "wid"), "hid"),
        P("section", "hid"),
        P("section", "wid"),
    )

    return jax.shard_map(
        shards,
        mesh=mesh,
        in_specs=placed,
        out_specs=(P(("section", "wid"), "hid"), P("section", "hid", "wid")),
        check_vma=False,
    )
```

```python
import jax
import jax.numpy as jnp
from jax import lax
from jax.experimental.layout import Layout, with_layout_constraint
from jax.sharding import PartitionSpec as P


D = 6144
FF = 24576


decay_rate = 0.9
root_half = 0.7071067811865476
inv_root_tau = 0.3989422804014327
LANES = 128


def normal_cdf(pre):
    return 0.5 * (1.0 + lax.erf(pre * root_half))


def gelu_value(pre):
    return pre * normal_cdf(pre)


def gelu_slope(pre):
    return normal_cdf(pre) + pre * jnp.exp(-0.5 * pre * pre) * inv_root_tau


def by_rows(block):
    return with_layout_constraint(block, Layout(major_to_minor=(0, 1)))


def contract(left, right):
    return lax.dot_general(
        left, right, (((0,), (0,)), ((), ())), preferred_element_type=jnp.float32
    )


def exchange(blocks, axis):
    return lax.all_to_all(blocks, axis, split_axis=0, concat_axis=0, tiled=True)


def spread(block, axis):
    n = lax.axis_size(axis)
    copies = jnp.broadcast_to(block[None], (n,) + block.shape)
    return exchange(copies.reshape((n * block.shape[0],) + block.shape[1:]), axis)


def thirds(values, scalar):
    shape = (16, values.shape[0])
    row = lax.broadcasted_iota(jnp.int32, shape, 0)
    rest = jnp.where(row < 8, jnp.broadcast_to(values[None], shape), scalar)
    out = jnp.zeros(shape, jnp.float32)
    for k in range(3):
        term = lax.reduce_precision(rest, exponent_bits=8, mantissa_bits=7)
        out = jnp.where(row % 8 == k, term, out)
        rest = rest - term
    return out.astype(jnp.bfloat16)


def scale_power(top):
    return jnp.clip(jnp.ceil(jnp.log2(jnp.maximum(top, 1e-30))), -96.0, 96.0)


def sum_blocks(partial, axis, groups):
    members = len(groups[0])
    columns = partial.shape[1]
    rows = partial.shape[0] // members
    power = scale_power(jnp.max(jnp.abs(partial)))
    coded = (partial * jnp.exp2(14.0 - power)).astype(jnp.float16).reshape(members, rows, columns)
    power = jnp.broadcast_to(power, (members, 8, columns)).astype(jnp.float16)
    taken = lax.all_to_all(
        jnp.concatenate([coded, power], axis=1),
        axis,
        split_axis=0,
        concat_axis=0,
        axis_index_groups=groups,
        tiled=True,
    )
    power = jnp.max(taken[:, rows:, :LANES].astype(jnp.float32), axis=(1, 2), keepdims=True)
    return jnp.sum(taken[:, :rows].astype(jnp.float32) * jnp.exp2(power - 14.0), axis=0)


def shards(weights, preact, inputs, grad_out, row_state, col_state):
    hid = lax.axis_size("hid")
    wid = lax.axis_size("wid")
    own_tile = weights[0]
    features, hidden = own_tile.shape
    half = hidden // 2
    rows = grad_out.shape[0]
    first = lax.axis_index("section") == 0
    even = lax.axis_index("hid") % 2 == 0
    home = lax.axis_index("section") == lax.axis_index("hid") % 2
    pair = ("section", "hid")

    def at(section, h):
        return section * hid + h

    over = [(at(h % 2, h), at(1 - h % 2, h)) for h in range(hid)]
    beside = [(at(h % 2, h ^ 1), at(h % 2, h)) for h in range(hid)]
    across = [(at(h % 2, h ^ 1), at(1 - h % 2, h)) for h in range(hid)]
    rings = [list(range(p, hid, 2)) for p in range(2)]

    def token_blocks(same, other):
        same, other = lax.optimization_barrier((same, other))
        far = lax.ppermute(other, pair, across)
        return same, lax.ppermute(other, pair, over), lax.ppermute(same, pair, beside), far

    def pick(blocks, columns):
        same, there, near, far = (block[:, columns] for block in blocks)
        return jnp.where(home, same, there), jnp.where(home, near, far)

    tile_near = lax.ppermute(
        own_tile[:, :half], pair, [(at(1, h), at(1, h ^ 1)) for h in range(hid)]
    )
    tile_over = lax.ppermute(own_tile[:, half:], pair, [(at(1, h), at(0, h)) for h in range(hid)])
    tile_far = lax.ppermute(
        own_tile[:, half:], pair, [(at(1, h), at(0, h ^ 1)) for h in range(hid)]
    )
    blocks = token_blocks(
        jnp.concatenate([grad_out, jnp.where(first, preact[:, half:], preact[:, :half])], axis=1),
        jnp.concatenate([grad_out, jnp.where(first, preact[:, :half], preact[:, half:])], axis=1),
    )
    grad_half = spread(jnp.concatenate(pick(blocks, slice(features)), axis=1), "wid")
    pre_own, pre_next = pick(blocks, slice(features, None))
    pre_half = jnp.concatenate(
        [jnp.where(even, pre_own, pre_next), jnp.where(even, pre_next, pre_own)]
    )
    pre_float = pre_half.astype(jnp.float32)
    act_half = gelu_value(pre_float).astype(jnp.bfloat16)
    acts = lax.all_gather(act_half, "hid", axis=0, tiled=True)
    hidden_part = jnp.dot(
        grad_half[:, :features],
        jnp.where(first, tile_over, own_tile[:, :half]),
        preferred_element_type=jnp.float32,
    ) + jnp.dot(
        grad_half[:, features:],
        jnp.where(first, tile_far, tile_near),
        preferred_element_type=jnp.float32,
    )
    hidden_share = sum_blocks(hidden_part, "hid", rings)
    hidden_share, acts = lax.optimization_barrier((hidden_share, acts))
    pre_share = (hidden_share * gelu_slope(pre_float)).astype(jnp.bfloat16)
    pre_share, up_left, down_left = lax.optimization_barrier((pre_share, inputs, grad_out))
    pres = lax.all_gather(pre_share, "hid", axis=0, tiled=True)

    def other_section(block):
        return lax.ppermute(block, "section", [(0, 1), (1, 0)])

    mine = jnp.concatenate([up_left, down_left], axis=1)
    taken = other_section(mine)
    tile_up = lax.ppermute(own_tile[:, :half], "section", [(0, 1)])
    left_own = jnp.concatenate([jnp.where(first, mine, taken), jnp.where(first, taken, mine)])
    left = jnp.swapaxes(
        spread(left_own, "wid").reshape(wid // 2, 2, 2, rows, 2 * features), 1, 2
    ).reshape(2 * wid * rows, 2 * features)

    def half_gradient(left_side, right_side):
        grad = by_rows(contract(left_side, right_side))
        squares = grad * grad
        row_sums, col_sums = jnp.sum(squares, axis=1), jnp.sum(squares, axis=0)
        return grad, row_sums, col_sums, scale_power(jnp.sqrt(jnp.sum(row_sums)))

    def coded(grad, power):
        return (grad * jnp.exp2(14.0 - power)).astype(jnp.float16)

    down = half_gradient(left[:, features:], acts)
    down_taken = lax.ppermute(coded(down[0], down[3]), "section", [(0, 1)])
    up = half_gradient(left[:, :features], pres)
    kept = [jnp.where(first, x, y) for x, y in zip(up, down)]
    given = [jnp.where(first, y, x) for x, y in zip(up[1:], down[1:])]
    sums = jnp.concatenate([given[1], given[0], jnp.broadcast_to(given[2], (LANES,))])
    sums = other_section(sums.reshape(-1, LANES)).reshape(-1)
    up_taken = lax.ppermute(coded(up[0], up[3]), "section", [(1, 0)])
    row_local = kept[1] + sums[half : half + features]
    col_local = jnp.concatenate(
        [jnp.where(first, sums[:half], kept[2]), jnp.where(first, kept[2], sums[:half])]
    )
    power = sums[half + features]
    row_prev = row_state[0]
    col_prev = col_state[0]
    scalars = jnp.stack([jnp.sum(row_local), jnp.sum(row_prev)])
    tail = jnp.concatenate([scalars, jnp.zeros((4 * LANES - 2,), jnp.float32)])
    packed = jnp.concatenate([col_local, tail]).reshape(-1, LANES)
    over_hid = jnp.sum(
        spread(packed, "hid").reshape((hid,) + packed.shape), axis=0
    ).reshape(-1)
    col_total = over_hid[:hidden]
    square_sum, prev_sum = over_hid[hidden], over_hid[hidden + 1]

    partial = lax.dot_general(
        pres,
        by_rows(jnp.where(first, own_tile[:, half:], tile_up)),
        (((1,), (1,)), ((), ())),
        preferred_element_type=jnp.float32,
    ).astype(jnp.bfloat16)
    blocks = jnp.swapaxes(partial.reshape(wid // 2, 2, 2, rows, features), 1, 2)
    extra = thirds(row_local, square_sum)
    blocks = jnp.concatenate(
        [blocks.reshape(wid, 2 * rows, features), jnp.broadcast_to(extra[None], (wid,) + extra.shape)],
        axis=1,
    )
    blocks = exchange(blocks, "wid")
    over_wid = jnp.sum(blocks.astype(jnp.float32), axis=0)
    low, high = over_wid[:rows], over_wid[rows : 2 * rows]
    input_sum = jnp.where(first, low, high) + other_section(jnp.where(first, high, low))
    input_grad = input_sum + grad_out.astype(jnp.float32)
    row_total = jnp.sum(over_wid[2 * rows : 2 * rows + 8], axis=0)
    square_total = jnp.sum(over_wid[2 * rows + 8 :, 0])

    swapped = jnp.where(first, up_taken, down_taken).astype(jnp.float32) * jnp.exp2(power - 14.0)
    gradient = jnp.concatenate(
        [jnp.where(first, swapped, kept[0]), jnp.where(first, kept[0], swapped)], axis=1
    )
    row_moment = decay_rate * row_prev + (1.0 - decay_rate) / FF * row_total
    col_moment = decay_rate * col_prev + (1.0 - decay_rate) / D * col_total
    row_mean = decay_rate / D * prev_sum + (1.0 - decay_rate) / FF / D * square_total
    update = gradient * lax.rsqrt(row_moment[:, None] * col_moment[None, :] / row_mean)
    return (input_grad, update[None])


def solution(mesh):
    placed = (
        P("section", "hid", "wid"),
        P(("section", "hid"), "wid"),
        P(("section", "wid"), "hid"),
        P(("section", "wid"), "hid"),
        P("section", "hid"),
        P("section", "wid"),
    )

    return jax.shard_map(
        shards,
        mesh=mesh,
        in_specs=placed,
        out_specs=(P(("section", "wid"), "hid"), P("section", "hid", "wid")),
        check_vma=False,
    )
```

```python
import jax
import jax.numpy as jnp
from jax import lax
from jax.sharding import PartitionSpec as P


D = 6144
FF = 24576


decay_rate = 0.9
root_half = 0.7071067811865476
inv_root_tau = 0.3989422804014327
LANES = 128


def normal_cdf(pre):
    return 0.5 * (1.0 + lax.erf(pre * root_half))


def gelu_value(pre):
    return pre * normal_cdf(pre)


def gelu_slope(pre):
    return normal_cdf(pre) + pre * jnp.exp(-0.5 * pre * pre) * inv_root_tau


def contract(left, right):
    return lax.dot_general(
        left, right, (((0,), (0,)), ((), ())), preferred_element_type=jnp.float32
    )


def exchange(blocks, axis):
    return lax.all_to_all(blocks, axis, split_axis=0, concat_axis=0, tiled=True)


def spread(block, axis):
    n = lax.axis_size(axis)
    copies = jnp.broadcast_to(block[None], (n,) + block.shape)
    return exchange(copies.reshape((n * block.shape[0],) + block.shape[1:]), axis)


def thirds(values, scalar):
    shape = (16, values.shape[0])
    row = lax.broadcasted_iota(jnp.int32, shape, 0)
    rest = jnp.where(row < 8, jnp.broadcast_to(values[None], shape), scalar)
    out = jnp.zeros(shape, jnp.float32)
    for k in range(3):
        term = lax.reduce_precision(rest, exponent_bits=8, mantissa_bits=7)
        out = jnp.where(row % 8 == k, term, out)
        rest = rest - term
    return out.astype(jnp.bfloat16)


def sum_blocks(partial, axis, groups):
    members = len(groups[0])
    columns = partial.shape[1]
    rows = partial.shape[0] // members
    power = jnp.clip(jnp.ceil(jnp.log2(jnp.maximum(jnp.max(jnp.abs(partial)), 1e-30))), -96.0, 96.0)
    coded = (partial * jnp.exp2(14.0 - power)).astype(jnp.float16).reshape(members, rows, columns)
    power = jnp.broadcast_to(power, (members, 8, columns)).astype(jnp.float16)
    taken = lax.all_to_all(
        jnp.concatenate([coded, power], axis=1),
        axis,
        split_axis=0,
        concat_axis=0,
        axis_index_groups=groups,
        tiled=True,
    )
    power = jnp.max(taken[:, rows:, :LANES].astype(jnp.float32), axis=(1, 2), keepdims=True)
    return jnp.sum(taken[:, :rows].astype(jnp.float32) * jnp.exp2(power - 14.0), axis=0)


def shards(weights, preact, inputs, grad_out, row_state, col_state):
    hid = lax.axis_size("hid")
    wid = lax.axis_size("wid")
    own_tile = weights[0]
    features, hidden = own_tile.shape
    half = hidden // 2
    rows = grad_out.shape[0]
    first = lax.axis_index("section") == 0
    even = lax.axis_index("hid") % 2 == 0
    home = lax.axis_index("section") == lax.axis_index("hid") % 2
    pair = ("section", "hid")

    def at(section, h):
        return section * hid + h

    over = [(at(h % 2, h), at(1 - h % 2, h)) for h in range(hid)]
    beside = [(at(h % 2, h ^ 1), at(h % 2, h)) for h in range(hid)]
    across = [(at(h % 2, h ^ 1), at(1 - h % 2, h)) for h in range(hid)]
    rings = [list(range(p, hid, 2)) for p in range(2)]

    def token_blocks(same, other):
        same, other = lax.optimization_barrier((same, other))
        far = lax.ppermute(other, pair, across)
        return same, lax.ppermute(other, pair, over), lax.ppermute(same, pair, beside), far

    def pick(blocks, columns):
        same, there, near, far = (block[:, columns] for block in blocks)
        return jnp.where(home, same, there), jnp.where(home, near, far)

    tile_near = lax.ppermute(
        own_tile[:, :half], pair, [(at(1, h), at(1, h ^ 1)) for h in range(hid)]
    )
    tile_over = lax.ppermute(own_tile[:, half:], pair, [(at(1, h), at(0, h)) for h in range(hid)])
    tile_far = lax.ppermute(
        own_tile[:, half:], pair, [(at(1, h), at(0, h ^ 1)) for h in range(hid)]
    )
    blocks = token_blocks(
        jnp.concatenate([grad_out, jnp.where(first, preact[:, half:], preact[:, :half])], axis=1),
        jnp.concatenate([grad_out, jnp.where(first, preact[:, :half], preact[:, half:])], axis=1),
    )
    grad_half = spread(jnp.concatenate(pick(blocks, slice(features)), axis=1), "wid")
    hidden_part = jnp.dot(
        grad_half[:, :features],
        jnp.where(first, tile_over, own_tile[:, :half]),
        preferred_element_type=jnp.float32,
    ) + jnp.dot(
        grad_half[:, features:],
        jnp.where(first, tile_far, tile_near),
        preferred_element_type=jnp.float32,
    )
    hidden_share = sum_blocks(hidden_part, "hid", rings)
    pre_own, pre_next = pick(blocks, slice(features, None))
    pre_half = jnp.concatenate(
        [jnp.where(even, pre_own, pre_next), jnp.where(even, pre_next, pre_own)]
    )
    pre_taken = lax.ppermute(pre_half, "section", [(0, 1)])
    act_share = gelu_value(
        jnp.concatenate([pre_half, pre_taken], axis=1).astype(jnp.float32)
    ).astype(jnp.bfloat16)
    pre_share = (hidden_share * gelu_slope(pre_half.astype(jnp.float32))).astype(jnp.bfloat16)
    pre_share = jnp.concatenate(
        [lax.ppermute(pre_share, "section", [(1, 0)]), pre_share], axis=1
    )
    right = lax.all_gather(jnp.where(first, pre_share, act_share), "hid", axis=0, tiled=True)

    kept = jnp.where(first, inputs, grad_out)
    given = jnp.where(first, grad_out, inputs)
    taken = lax.ppermute(given, "section", [(0, 1), (1, 0)])
    left_own = jnp.concatenate([jnp.where(first, kept, taken), jnp.where(first, taken, kept)])
    left = jnp.swapaxes(
        spread(left_own, "wid").reshape(wid // 2, 2, 2, rows, features), 1, 2
    ).reshape(2 * wid * rows, features)

    gradient = contract(left, right)
    squares = gradient * gradient
    row_local = jnp.sum(squares, axis=1)
    col_local = jnp.sum(squares, axis=0)
    row_prev = row_state[0]
    col_prev = col_state[0]
    scalars = jnp.stack([jnp.sum(row_local), jnp.sum(row_prev)])
    tail = jnp.concatenate([scalars, jnp.zeros((4 * LANES - 2,), jnp.float32)])
    packed = jnp.concatenate([col_local, tail]).reshape(-1, LANES)
    over_hid = jnp.sum(
        spread(packed, "hid").reshape((hid,) + packed.shape), axis=0
    ).reshape(-1)
    col_total = over_hid[:hidden]
    square_sum, prev_sum = over_hid[hidden], over_hid[hidden + 1]

    partial = lax.dot_general(
        right, own_tile, (((1,), (1,)), ((), ())), preferred_element_type=jnp.float32
    ).astype(jnp.bfloat16)
    blocks = jnp.swapaxes(partial.reshape(wid // 2, 2, 2, rows, features), 1, 2)
    extra = thirds(row_local, square_sum)
    blocks = jnp.concatenate(
        [blocks.reshape(wid, 2 * rows, features), jnp.broadcast_to(extra[None], (wid,) + extra.shape)],
        axis=1,
    )
    over_wid = jnp.sum(exchange(blocks, "wid").astype(jnp.float32), axis=0)
    input_sum = jnp.where(
        first, over_wid[:rows], lax.ppermute(over_wid[rows : 2 * rows], "section", [(0, 1)])
    )
    input_grad = input_sum + grad_out.astype(jnp.float32)
    row_total = jnp.sum(over_wid[2 * rows : 2 * rows + 8], axis=0)
    square_total = jnp.sum(over_wid[2 * rows + 8 :, 0])

    row_moment = decay_rate * row_prev + (1.0 - decay_rate) / FF * row_total
    col_moment = decay_rate * col_prev + (1.0 - decay_rate) / D * col_total
    row_mean = decay_rate / D * prev_sum + (1.0 - decay_rate) / FF / D * square_total
    update = gradient * lax.rsqrt(row_moment[:, None] * col_moment[None, :] / row_mean)
    return (input_grad, update[None])


def solution(mesh):
    placed = (
        P("section", "hid", "wid"),
        P(("section", "hid"), "wid"),
        P(("section", "wid"), "hid"),
        P(("section", "wid"), "hid"),
        P("section", "hid"),
        P("section", "wid"),
    )

    return jax.shard_map(
        shards,
        mesh=mesh,
        in_specs=placed,
        out_specs=(P(("section", "wid"), "hid"), P("section", "hid", "wid")),
        check_vma=False,
    )
```
